32 devices in a mesh: fsdp: 4 (over z), ctx: 4 (over x, core), tp: 2 (over y).
Axes of the slice: x: 2, y: 2, z: 4, core: 2. Of those that a mesh axis runs over, the one named last changes fastest.
Arguments:
- tokens: bfloat16 [4, 2048, 1536], P('fsdp', 'ctx'), may hold values from -25 to 25
- lengths: int32 [4], P('fsdp'), may hold values from 512 to 2048, as said below
- routes: int32 [4, 2048, 8], P('fsdp', 'ctx'), may hold values from 0 to 15, all different within a row
- visit_order: int32 [4, 4, 4096], P('fsdp', 'ctx'), may hold values from 0 to 4095, each once within a row
- cotangent: bfloat16 [4, 2048, 1536], P('fsdp', 'ctx'), may hold values from -6 to 6
- first_gain: bfloat16 [1536], P('fsdp'), may hold values from 0.099609375 to 1.8984375
- query_weight: bfloat16 [1536, 1536], P('fsdp', 'tp'), may hold values from -0.15625 to 0.15625
- key_matrix: bfloat16 [1536, 512], P('fsdp', 'tp'), may hold values from -0.15625 to 0.15625
- value_matrix: bfloat16 [1536, 512], P('fsdp', 'tp'), may hold values from -0.15625 to 0.15625
- output_weight: bfloat16 [1536, 1536], P('tp', 'fsdp'), may hold values from -3.5 to 3.5
- second_gain: bfloat16 [1536], P('fsdp'), may hold values from 0.099609375 to 1.8984375
- router_weight: bfloat16 [1536, 16], P('fsdp'), may hold values from -0.078125 to 0.078125
- gate_weight: bfloat16 [16, 1536, 512], P('fsdp', None, 'tp'), may hold values from -0.15625 to 0.15625
- up_weight: bfloat16 [16, 1536, 512], P('fsdp', None, 'tp'), may hold values from -0.15625 to 0.15625
- down_weight: bfloat16 [16, 512, 1536], P('fsdp', 'tp'), may hold values from -0.75 to 0.75
Outputs:
- layer_out: bfloat16 [4, 2048, 1536], P('fsdp', 'ctx')
- grad_tokens: float32 [4, 2048, 1536], P('fsdp', 'ctx')
- grad_first_gain: float32 [1536], P('fsdp')
- grad_query_weight: float32 [1536, 1536], P('fsdp', 'tp')
- grad_key_weight: float32 [1536, 512], P('fsdp', 'tp')
- grad_value_weight: float32 [1536, 512], P('fsdp', 'tp')
- grad_output_weight: float32 [1536, 1536], P('tp', 'fsdp')
- grad_second_gain: float32 [1536], P('fsdp')
- grad_router_weight: float32 [1536, 16], P('fsdp')
- grad_gate_weight: float32 [16, 1536, 512], P('fsdp', None, 'tp')
- grad_up_weight: float32 [16, 1536, 512], P('fsdp', None, 'tp')
- grad_down_weight: float32 [16, 512, 1536], P('fsdp', 'tp')
The draws below stay inside these ranges and needn't reach their ends.
Inputs may be any that keep to these rules, and one draw needn't show every extreme that they name: `lengths`: in every draw some sequence has length 2048. `routes`: the 8 experts of a token are different. `visit_order`: for each sequence and block, the entries are a permutation of the block's pair numbers.
All inputs are finite; a program needn't handle non-finite values.
Results may differ from the reference program's by a relative error of at most 0.028.
Values may be sent and summed in bfloat16 or wider, within the bound.
No kernel may reach another device: no remote copies, remote signals or barrier semaphores. Data moves between devices by JAX's collectives and lax.ppermute only.
A program may use at most 256 MiB of HBM per device.

```python
import math
import jax
import jax.numpy as jnp
from jax import lax

MODEL_WIDTH = 1536
QUERY_HEADS = 24
KEY_VALUE_HEADS = 8
HEAD_SIZE = 64
F = 512
TOPK = 8
E = 16
SCORE_BLOCK = 512
SEQ_DEV = 512
PADDED_LENGTH = 2048
SEQS = 4
CAP = 256
N_CTX = 4
N_TP = 2


def draw_tokens(key, part):
    first_key = jax.random.fold_in(key, 21)
    second_key = jax.random.fold_in(key, 22)
    third_key = jax.random.fold_in(key, 23)
    base_values = jnp.clip(jax.random.normal(first_key, (SEQS, PADDED_LENGTH, MODEL_WIDTH), jnp.float32), -4.0, 4.0)
    row_scale = jnp.exp(jax.random.uniform(second_key, (SEQS, PADDED_LENGTH, 1), jnp.float32, -0.9, 0.9))
    column_scale = jnp.exp(jax.random.uniform(third_key, (MODEL_WIDTH,), jnp.float32, -0.9, 0.9))
    return (base_values * row_scale * column_scale).astype(jnp.bfloat16)


def draw_lengths(key, part):
    spread = jax.random.randint(jax.random.fold_in(key, 11), (SEQS,), PADDED_LENGTH // 4, PADDED_LENGTH + 1)
    chosen = jax.random.randint(jax.random.fold_in(key, 12), (), 0, SEQS)
    return jnp.where(jnp.arange(SEQS) == chosen, PADDED_LENGTH, spread).astype(jnp.int32)


def block_levels(key, shape, split, smallest, top_value):
    level, own = 1.0, jax.random.fold_in(key, 6)
    for position, parts in split:
        draws = jnp.exp(jax.random.uniform(jax.random.fold_in(own, position), (parts,), jnp.float32, smallest / len(split), top_value / len(split)))
        level = level * jnp.repeat(draws, shape[position] // parts).reshape([-1 if axis == position else 1 for axis in range(len(shape))])
    return level


def distinct(stream_key, rows, number_of, top, lift):
    sequence = jax.random.permutation(jax.random.fold_in(stream_key, 1), number_of)
    boost = sequence
    for power in range(3):
        boost = boost * boost // number_of
    boost = boost * lift // number_of
    tickets = jax.random.randint(jax.random.fold_in(stream_key, 2), (rows, number_of), 0, 4096) + boost
    fixed_rows = jax.random.permutation(jax.random.fold_in(stream_key, 3), rows)[jnp.arange(number_of) % rows]
    tickets = jnp.where(jnp.arange(rows)[:, None] == fixed_rows[None, :], 1 << 14, tickets)
    score = tickets * number_of + jnp.arange(number_of)
    return lax.top_k(score.astype(jnp.int32), top)[1].astype(jnp.int32)


def noise(key, dims, scale, bound, pieces=(), held_as=jnp.bfloat16):
    entries = jax.random.normal(key, dims, jnp.float32) * scale
    if len(pieces) > 0:
        entries = block_levels(key, dims, pieces, -0.22, 0.18) * entries
    return jnp.clip(entries, min=-bound, max=bound).astype(held_as)


def setup_inputs(seed: int = 0) -> dict:
    splits = jax.random.split(jax.random.key(seed), 16)
    tokens = draw_tokens(jax.random.fold_in(splits[15], 71), 0)
    lengths = draw_lengths(jax.random.fold_in(splits[15], 71), 0)
    routes = distinct(splits[2], SEQS * PADDED_LENGTH, E, TOPK, 4096).reshape((SEQS, PADDED_LENGTH, TOPK))
    visit_order = jax.vmap(lambda own: jax.random.permutation(own, SEQ_DEV * TOPK))(jax.random.split(splits[3], SEQS * N_CTX)).reshape((SEQS, N_CTX, SEQ_DEV * TOPK)).astype(jnp.int32)
    cotangent = noise(splits[4], (SEQS, PADDED_LENGTH, MODEL_WIDTH), 1.0, 6.0, ((0, 4), (1, 4)))
    first_gain = jnp.clip(1.0 + 0.18 * jax.random.normal(splits[5], (MODEL_WIDTH,), jnp.float32), 0.099609375, 1.8984375).astype(jnp.bfloat16)
    query_weight = noise(splits[6], (MODEL_WIDTH, QUERY_HEADS * HEAD_SIZE), MODEL_WIDTH ** -0.5, 0.15625, ((0, 4), (1, 2)))
    key_matrix = noise(splits[7], (MODEL_WIDTH, KEY_VALUE_HEADS * HEAD_SIZE), MODEL_WIDTH ** -0.5, 0.15625, ((0, 4), (1, 2)))
    value_matrix = noise(splits[8], (MODEL_WIDTH, KEY_VALUE_HEADS * HEAD_SIZE), MODEL_WIDTH ** -0.5, 0.15625, ((0, 4), (1, 2)))
    output_weight = noise(splits[9], (QUERY_HEADS * HEAD_SIZE, MODEL_WIDTH), (max(QUERY_HEADS * HEAD_SIZE // 512, 1)) ** -0.5, 3.5, ((0, 2), (1, 4)))
    second_gain = jnp.clip(1.0 + 0.18 * jax.random.normal(splits[10], (MODEL_WIDTH,), jnp.float32), 0.099609375, 1.8984375).astype(jnp.bfloat16)
    router_weight = noise(splits[11], (MODEL_WIDTH, E), (4 * MODEL_WIDTH) ** -0.5, 0.078125, ((0, 4),))
    gate_weight = noise(splits[12], (E, MODEL_WIDTH, F), MODEL_WIDTH ** -0.5, 0.15625, ((0, 4), (2, 2)))
    up_weight = noise(splits[13], (E, MODEL_WIDTH, F), MODEL_WIDTH ** -0.5, 0.15625, ((0, 4), (2, 2)))
    down_weight = noise(splits[14], (E, F, MODEL_WIDTH), (max(F // 8, 1)) ** -0.5, 0.75, ((0, 4), (1, 2)))
    return dict(tokens=tokens, lengths=lengths, routes=routes, visit_order=visit_order, cotangent=cotangent, first_gain=first_gain, query_weight=query_weight, key_matrix=key_matrix, value_matrix=value_matrix, output_weight=output_weight, second_gain=second_gain, router_weight=router_weight, gate_weight=gate_weight, up_weight=up_weight, down_weight=down_weight)


EPSILON = 1e-06
PRECISE = lax.Precision.HIGHEST

@jax.custom_vjp
def low(v):
    return lax.optimization_barrier(v.astype(jnp.bfloat16)).astype(jnp.float32)

@jax.custom_vjp
def low_back(v):
    return v

def low_keep(v):
    return (low(v), None)

def low_pass(kept, grad):
    return (grad,)

def back_keep(v):
    return (v, None)

def back_low(kept, grad):
    return (low(grad),)
low.defvjp(low_keep, low_pass)
low_back.defvjp(back_keep, back_low)

def matmul(left, right):
    return jnp.dot(left, right, precision=PRECISE, preferred_element_type=jnp.float32)

def rms_normed(values):
    return values * lax.rsqrt(lax.optimization_barrier(jnp.mean(values * values, axis=-1, keepdims=True)) + EPSILON)

def rotation_tables(positions):
    half_dim = HEAD_SIZE // 2
    frequency = jnp.exp(jnp.arange(half_dim, dtype=jnp.float32) * (-2.0 * math.log(10000.0) / HEAD_SIZE))
    angles = positions.astype(jnp.float32)[:, None] * frequency[None, :]
    return (jnp.cos(angles)[:, None, :], jnp.sin(angles)[:, None, :])

def rotate(values, cosine_table, sine_table):
    row_count = values.shape[0]
    head_count = values.shape[1] // HEAD_SIZE
    shaped = values.reshape(row_count, head_count, HEAD_SIZE)
    first_half = shaped[:, :, :HEAD_SIZE // 2]
    second_half = shaped[:, :, HEAD_SIZE // 2:]
    joined = jnp.concatenate([first_half * cosine_table - second_half * sine_table, second_half * cosine_table + first_half * sine_table], axis=-1)
    return joined.reshape(row_count, head_count * HEAD_SIZE)

def plan_block(route_rows, ranked, live_rows):
    pair_count = route_rows.shape[0] * route_rows.shape[1]
    pair_expert = route_rows.reshape(-1)
    pair_live = jnp.repeat(live_rows, route_rows.shape[1])
    ranked_expert = pair_expert[ranked]
    ranked_live = pair_live[ranked]
    expert_hits = ((ranked_expert[:, None] == jnp.arange(E, dtype=jnp.int32)[None, :]) & ranked_live[:, None]).astype(jnp.int32)
    earlier = jnp.cumsum(expert_hits, axis=0) - expert_hits
    slot_place = lax.optimization_barrier(jnp.sum(earlier * expert_hits, axis=1))
    is_kept = ranked_live & (slot_place < CAP)
    slot_index = jnp.where(is_kept, ranked_expert * CAP + slot_place, E * CAP).astype(jnp.int32)
    slot_pair = jnp.full((E * CAP + 1,), pair_count, jnp.int32).at[slot_index].set(ranked.astype(jnp.int32))[:E * CAP]
    pair_slot = jnp.full((pair_count,), E * CAP, jnp.int32).at[ranked].set(slot_index)
    return (slot_pair, pair_slot)

def take_rows(table, index_rows):
    return table[index_rows]

def sequence_layer(weights, inputs, length, route_rows, slot_pair, pair_slot):
    first_gain, query_weight, key_matrix, value_matrix, output_weight, second_gain, router_weight, gate_weight, up_weight, down_weight = weights
    positions = jnp.arange(PADDED_LENGTH, dtype=jnp.int32)
    valid = (positions < length).astype(jnp.float32)[:, None]
    cosine_table, sine_table = rotation_tables(positions)
    hidden_one = low(rms_normed(inputs) * first_gain)
    query_rows = low(rotate(low_back(matmul(hidden_one, query_weight)), cosine_table, sine_table))
    rotated_keys = low(rotate(low_back(matmul(hidden_one, key_matrix)), cosine_table, sine_table))
    every_value = low(low_back(matmul(hidden_one, value_matrix)))
    heads_per_group = QUERY_HEADS // KEY_VALUE_HEADS
    query_block_list = query_rows.reshape(PADDED_LENGTH // SCORE_BLOCK, SCORE_BLOCK, KEY_VALUE_HEADS, heads_per_group, HEAD_SIZE)
    key_head_rows = rotated_keys.reshape(PADDED_LENGTH, KEY_VALUE_HEADS, HEAD_SIZE)
    value_head_rows = every_value.reshape(PADDED_LENGTH, KEY_VALUE_HEADS, HEAD_SIZE)
    score_scale = HEAD_SIZE ** (-0.5)

    def attend_block(item):
        block_index, query_block = item
        query_pos = block_index * SCORE_BLOCK + jnp.arange(SCORE_BLOCK, dtype=jnp.int32)
        scores = low_back(jnp.einsum('qhgd,khd->hgqk', query_block, key_head_rows, precision=PRECISE, preferred_element_type=jnp.float32) * score_scale)
        allowed = (positions[None, :] <= query_pos[:, None]) & (positions[None, :] < length)
        probs = jax.nn.softmax(jnp.where(allowed, scores, -jnp.inf), axis=-1)
        return jnp.einsum('hgqk,khd->qhgd', low(probs), value_head_rows, precision=PRECISE, preferred_element_type=jnp.float32)
    attended = lax.map(jax.checkpoint(attend_block), (jnp.arange(PADDED_LENGTH // SCORE_BLOCK, dtype=jnp.int32), query_block_list))
    attended = low(low_back(attended.reshape(PADDED_LENGTH, QUERY_HEADS * HEAD_SIZE)))
    residual = inputs + low_back(matmul(attended, output_weight))
    hidden_two = low(rms_normed(residual) * second_gain)
    logits = low_back(matmul(hidden_two, router_weight))
    route_onehot = (route_rows[:, :, None] == jnp.arange(E, dtype=jnp.int32)[None, None, :]).astype(jnp.float32)
    gate_weights = jax.nn.softmax(lax.optimization_barrier(jnp.sum(route_onehot * logits[:, None, :], axis=-1)), axis=-1)
    slot_token = slot_pair // TOPK
    hidden_blocks = hidden_two.reshape(N_CTX, SEQ_DEV, MODEL_WIDTH)
    hidden_pad = jnp.concatenate([hidden_blocks, jnp.zeros((N_CTX, 1, MODEL_WIDTH), jnp.float32)], axis=1)
    dispatched = jax.vmap(take_rows)(hidden_pad, slot_token).reshape(N_CTX, E, CAP, MODEL_WIDTH)
    group_width = F // N_TP
    mixture = jnp.zeros((PADDED_LENGTH, MODEL_WIDTH), jnp.float32)
    for group_index in range(N_TP):
        low_col = group_index * group_width
        expert_in = low_back(dispatched)
        gate_pre = low_back(jnp.einsum('becd,edf->becf', expert_in, gate_weight[:, :, low_col:low_col + group_width], precision=PRECISE, preferred_element_type=jnp.float32))
        up_pre = low_back(jnp.einsum('becd,edf->becf', expert_in, up_weight[:, :, low_col:low_col + group_width], precision=PRECISE, preferred_element_type=jnp.float32))
        hidden_mid = low(jax.nn.silu(gate_pre) * up_pre)
        produced = low(low_back(jnp.einsum('becf,efd->becd', hidden_mid, down_weight[:, low_col:low_col + group_width, :], precision=PRECISE, preferred_element_type=jnp.float32)))
        produced_pad = jnp.concatenate([produced.reshape(N_CTX, E * CAP, MODEL_WIDTH), jnp.zeros((N_CTX, 1, MODEL_WIDTH), jnp.float32)], axis=1)
        pair_out = jax.vmap(take_rows)(produced_pad, pair_slot).reshape(PADDED_LENGTH, TOPK, MODEL_WIDTH)
        mixture = mixture + lax.optimization_barrier(jnp.sum(gate_weights[:, :, None] * pair_out, axis=1))
    return valid * (residual + mixture)

def reference(tokens, lengths, routes, visit_order, cotangent, first_gain, query_weight, key_matrix, value_matrix, output_weight, second_gain, router_weight, gate_weight, up_weight, down_weight):
    live_all = jnp.arange(PADDED_LENGTH, dtype=jnp.int32)[None, :] < lengths[:, None]
    route_blocks = routes.reshape(SEQS, N_CTX, SEQ_DEV, TOPK)
    live_blocks = live_all.reshape(SEQS, N_CTX, SEQ_DEV)
    slot_pair, pair_slot = jax.vmap(jax.vmap(plan_block))(route_blocks, visit_order, live_blocks)
    weights = (first_gain.astype(jnp.float32), query_weight.astype(jnp.float32), key_matrix.astype(jnp.float32), value_matrix.astype(jnp.float32), output_weight.astype(jnp.float32), second_gain.astype(jnp.float32), router_weight.astype(jnp.float32), gate_weight.astype(jnp.float32), up_weight.astype(jnp.float32), down_weight.astype(jnp.float32))

    def forward(all_inputs, weight_set):

        def one_sequence(item):
            inputs, length, route_rows, slot_rows, pair_rows = item
            return sequence_layer(weight_set, inputs, length, route_rows, slot_rows, pair_rows)
        return lax.map(jax.checkpoint(one_sequence), (all_inputs, lengths, routes, slot_pair, pair_slot))
    layer_out, pullback = jax.vjp(forward, tokens.astype(jnp.float32), weights)
    grad_inputs, grad_weights = pullback(cotangent.astype(jnp.float32))
    return (layer_out.astype(jnp.bfloat16), grad_inputs, grad_weights[0], grad_weights[1], grad_weights[2], grad_weights[3], grad_weights[4], grad_weights[5], grad_weights[6], grad_weights[7], grad_weights[8], grad_weights[9])
```

```python
import functools
import math

import jax
import jax.numpy as jnp
from jax import lax
from jax.experimental import pallas as pl
from jax.experimental.pallas import tpu as pltpu
from jax.sharding import PartitionSpec as P

HEAD_SIZE = 64
HALF_HEAD = 32
TOPK = 8
E = 16
CAP = 256
EPSILON = 1e-06
LANES = 128
NEGATIVE = -1e30
FAR = 1e9


BF = jnp.bfloat16
F32 = jnp.float32


def mm(a, b):
    return lax.dot_general(a, b, (((1,), (0,)), ((), ())), preferred_element_type=F32)


def mm_nt(a, b):
    return lax.dot_general(a, b, (((1,), (1,)), ((), ())), preferred_element_type=F32)


def mm_tn(a, b):
    return lax.dot_general(a, b, (((0,), (0,)), ((), ())), preferred_element_type=F32)


def vmem():
    return pl.BlockSpec(memory_space=pltpu.VMEM)


def smem():
    return pl.BlockSpec(memory_space=pltpu.SMEM)


def cost(flops, nbytes, transcendentals=0):
    return pl.CostEstimate(
        flops=int(flops), bytes_accessed=int(nbytes), transcendentals=int(transcendentals)
    )


def plan_kernel(info, visit_ref, route_ref, table_ref):
    rows = route_ref.shape[1]
    pairs = visit_ref.shape[1]
    visit = visit_ref[...]
    token = visit >> 3
    choice = visit & 7
    place = lax.broadcasted_iota(jnp.int32, (1, pairs), 1)
    line = lax.broadcasted_iota(jnp.int32, (16, pairs), 0)
    weight = jnp.where(line < 8, place >> 6, place & 63).astype(F32)
    left = jnp.where((line & 7) == choice, weight, 0.0).astype(BF)
    rank = jnp.zeros((16, rows), F32)
    step = 512
    for start in range(0, pairs, step):
        hot = lax.broadcasted_iota(jnp.int32, (rows, step), 0) == token[:, start : start + step]
        rank = rank + mm_nt(left[:, start : start + step], jnp.where(hot, 1.0, 0.0).astype(BF))
    rank = rank[:8] * 64.0 + rank[8:]
    first_row = info[0]
    length = info[1]
    live = (lax.broadcasted_iota(jnp.int32, (1, rows), 1) + first_row) < length
    route = route_ref[...]
    order_rows = []
    chosen_rows = []
    for e in range(E):
        match = route == e
        chosen = jnp.max(jnp.where(match, 1.0, 0.0), axis=0, keepdims=True) > 0.5
        order = jnp.sum(jnp.where(match, rank, 0.0), axis=0, keepdims=True)
        order_rows.append(jnp.where(chosen & live, order, FAR))
        chosen_rows.append(chosen)
    stacked = jnp.concatenate(order_rows + [jnp.zeros((LANES - E, rows), F32)], axis=0)
    turned = stacked.T
    for e in range(E):
        earlier = jnp.where(turned[:, e : e + 1] < order_rows[e], 1.0, 0.0)
        count = jnp.sum(earlier, axis=0, keepdims=True)
        kept = (order_rows[e] < FAR) & (count < CAP)
        table_ref[e : e + 1, :] = jnp.where(
            chosen_rows[e], jnp.where(kept, count, -1.0), -2.0
        )


def make_plan(info, visit, route_t):
    rows = route_t.shape[1]
    return pl.pallas_call(
        plan_kernel,
        out_shape=jax.ShapeDtypeStruct((E, rows), F32),
        in_specs=[smem(), vmem(), vmem()],
        out_specs=vmem(),
        cost_estimate=cost(16 * 4096 * 512 * 2 + 4e6, 1e5),
        name="plan",
    )(info, visit, route_t)


def spin(values, cosine, sine):
    width = values.shape[1]
    lane = lax.broadcasted_iota(jnp.int32, values.shape, 1)
    low = (lane & (HEAD_SIZE - 1)) < HALF_HEAD
    other = jnp.where(
        low, pltpu.roll(values, width - HALF_HEAD, 1), pltpu.roll(values, HALF_HEAD, 1)
    )
    return values * cosine + other * sine


def project_kernel(x_ref, gain_ref, w_ref, cos_ref, sin_ref, h_ref, q_ref, kv_ref):
    x = x_ref[...].astype(F32)
    inverse = lax.rsqrt(jnp.mean(x * x, axis=-1, keepdims=True) + EPSILON)
    h_ref[...] = (x * inverse * gain_ref[...]).astype(BF)
    h = h_ref[...]
    cosine = cos_ref[...]
    sine = sin_ref[...]
    q_half = q_ref.shape[1] // 2
    kv_half = kv_ref.shape[1] // 2
    for half in range(2):
        out = mm(h, w_ref[half])
        for j in range(0, q_half, LANES):
            q_ref[:, half * q_half + j : half * q_half + j + LANES] = (
                spin(out[:, j : j + LANES], cosine, sine) * HEAD_SIZE ** (-0.5)
            ).astype(BF)
        k_width = kv_half // 2
        for j in range(0, k_width, LANES):
            kv_ref[:, half * kv_half + j : half * kv_half + j + LANES] = spin(
                out[:, q_half + j : q_half + j + LANES], cosine, sine
            ).astype(BF)
        kv_ref[:, half * kv_half + k_width : (half + 1) * kv_half] = out[
            :, q_half + k_width :
        ].astype(BF)


def project(x, gain, w, cosine, sine, q_width, kv_width):
    rows, width = x.shape
    return pl.pallas_call(
        project_kernel,
        out_shape=(
            jax.ShapeDtypeStruct((rows, width), BF),
            jax.ShapeDtypeStruct((rows, q_width), BF),
            jax.ShapeDtypeStruct((rows, kv_width), BF),
        ),
        in_specs=[vmem()] * 5,
        out_specs=(vmem(),) * 3,
        cost_estimate=cost(2 * rows * width * (q_width + kv_width), 9e6),
        name="project",
    )(x, gain, w, cosine, sine)


def head_lanes(g):
    base = (g // 2) * 4 * HEAD_SIZE + (g % 2) * HEAD_SIZE
    return base, base + 2 * HEAD_SIZE


def attend_kernel(info, *refs, blocks, tp_rows):
    q_ref = refs[0]
    kv_refs = refs[1 : 1 + blocks]
    wo_ref = refs[1 + blocks]
    o_ref, lse_ref, mine_ref, other_ref = refs[2 + blocks : 6 + blocks]
    kv_scr, lse_scr = refs[6 + blocks :]
    rows = q_ref.shape[0]
    heads = q_ref.shape[1] // HEAD_SIZE
    kv_heads = kv_refs[0].shape[1] // (2 * HEAD_SIZE)
    group = heads // kv_heads
    block = info[0]
    length = info[1]
    tp_index = info[2]
    for j in range(blocks):
        kv_scr[pl.ds(pl.multiple_of(info[3 + j] * rows, rows), rows), :] = kv_refs[j][...]
    count = jnp.minimum(block + 1, (length + rows - 1) // rows)
    query_pos = block * rows + lax.broadcasted_iota(jnp.int32, (rows, 1), 0)
    bound = jnp.minimum(query_pos, length - 1)
    key_lane = lax.broadcasted_iota(jnp.int32, (1, rows), 1)
    lse_scr[...] = jnp.zeros_like(lse_scr)
    for h in range(heads):
        k_lane, v_lane = head_lanes(h // group)
        q = q_ref[:, h * HEAD_SIZE : (h + 1) * HEAD_SIZE]

        def step(kb, carry):
            top, total, acc = carry
            base = pl.multiple_of(kb * rows, rows)
            k = kv_scr[pl.ds(base, rows), k_lane : k_lane + HEAD_SIZE]
            v = kv_scr[pl.ds(base, rows), v_lane : v_lane + HEAD_SIZE]
            s = mm_nt(q, k)
            s = jnp.where(key_lane + base <= bound, s, NEGATIVE)
            new_top = jnp.maximum(top, jnp.max(s, axis=1, keepdims=True))
            p = jnp.exp(s - new_top)
            fade = jnp.exp(top - new_top)
            total = total * fade + jnp.sum(p, axis=1, keepdims=True)
            acc = acc * fade + mm(p.astype(BF), v)
            return new_top, total, acc

        top, total, acc = lax.fori_loop(
            0,
            count,
            step,
            (
                jnp.full((rows, 1), NEGATIVE, F32),
                jnp.zeros((rows, 1), F32),
                jnp.zeros((rows, HEAD_SIZE), F32),
            ),
        )
        o_ref[:, h * HEAD_SIZE : (h + 1) * HEAD_SIZE] = (acc / total).astype(BF)
        lse_scr[:, h : h + 1] = top + jnp.log(total)
    lse_ref[...] = lse_scr[...].T[: lse_ref.shape[0], :]
    wo = wo_ref[...]
    mine_ref[...] = mm(o_ref[pl.ds(pl.multiple_of(tp_index * tp_rows, tp_rows), tp_rows), :], wo)
    other_ref[...] = mm(
        o_ref[pl.ds(pl.multiple_of((1 - tp_index) * tp_rows, tp_rows), tp_rows), :], wo
    ).astype(BF)


def attend(info, q, kv_blocks, wo):
    rows, q_width = q.shape
    width = wo.shape[1]
    blocks = len(kv_blocks)
    kv_width = kv_blocks[0].shape[1]
    half = rows // 2
    heads = q_width // HEAD_SIZE
    return pl.pallas_call(
        functools.partial(attend_kernel, blocks=blocks, tp_rows=half),
        out_shape=(
            jax.ShapeDtypeStruct((rows, q_width), BF),
            jax.ShapeDtypeStruct((16, rows), F32),
            jax.ShapeDtypeStruct((half, width), F32),
            jax.ShapeDtypeStruct((half, width), BF),
        ),
        in_specs=[smem()] + [vmem()] * (2 + blocks),
        out_specs=(vmem(),) * 4,
        scratch_shapes=[
            pltpu.VMEM((blocks * rows, kv_width), BF),
            pltpu.VMEM((rows, LANES), F32),
        ],
        cost_estimate=cost(4 * rows * rows * blocks * q_width * 4, 8e6, heads * rows * rows * blocks),
        name="attend",
    )(info, q, *kv_blocks, wo)


def attend_back_kernel(info, *refs, blocks, tp_rows):
    q_ref = refs[0]
    kv_refs = refs[1 : 1 + blocks]
    wo_ref, o_ref, lse_ref, mine_ref, other_ref, cos_ref, sin_ref = refs[1 + blocks : 8 + blocks]
    dq_ref = refs[8 + blocks]
    dkv_refs = refs[9 + blocks : 9 + 2 * blocks]
    kv_scr, dkv_scr, da_scr, do_scr, dq_scr = refs[9 + 2 * blocks :]
    rows = q_ref.shape[0]
    heads = q_ref.shape[1] // HEAD_SIZE
    kv_heads = kv_refs[0].shape[1] // (2 * HEAD_SIZE)
    group = heads // kv_heads
    block = info[0]
    length = info[1]
    tp_index = info[2]
    da_scr[pl.ds(pl.multiple_of(tp_index * tp_rows, tp_rows), tp_rows), :] = mine_ref[...]
    da_scr[pl.ds(pl.multiple_of((1 - tp_index) * tp_rows, tp_rows), tp_rows), :] = other_ref[...]
    for j in range(blocks):
        kv_scr[pl.ds(pl.multiple_of(info[3 + j] * rows, rows), rows), :] = kv_refs[j][...]
    dkv_scr[...] = jnp.zeros_like(dkv_scr)
    do_scr[...] = mm_nt(da_scr[...], wo_ref[...]).astype(BF)
    q_width = q_ref.shape[1]
    picker = (
        lax.broadcasted_iota(jnp.int32, (16, q_width), 1) // HEAD_SIZE
        == lax.broadcasted_iota(jnp.int32, (16, q_width), 0)
    )
    delta = lax.dot_general(
        jnp.where(picker, 1.0, 0.0),
        do_scr[...].astype(F32) * o_ref[...].astype(F32),
        (((1,), (1,)), ((), ())),
        precision=lax.Precision.HIGHEST,
        preferred_element_type=F32,
    )
    lse = lse_ref[...]
    count = jnp.minimum(block + 1, (length + rows - 1) // rows)
    query_pos = block * rows + lax.broadcasted_iota(jnp.int32, (1, rows), 1)
    bound = jnp.minimum(query_pos, length - 1)
    bound = jnp.concatenate([bound] * group, axis=1)
    key_line = lax.broadcasted_iota(jnp.int32, (rows, 1), 0)
    for g in range(kv_heads):
        k_lane, v_lane = head_lanes(g)
        lo = g * group
        q = jnp.concatenate(
            [q_ref[:, (lo + i) * HEAD_SIZE : (lo + i + 1) * HEAD_SIZE] for i in range(group)],
            axis=0,
        )
        do = jnp.concatenate(
            [do_scr[:, (lo + i) * HEAD_SIZE : (lo + i + 1) * HEAD_SIZE] for i in range(group)],
            axis=0,
        )
        shift = jnp.concatenate([lse[lo + i : lo + i + 1] for i in range(group)], axis=1)
        slope = jnp.concatenate([delta[lo + i : lo + i + 1] for i in range(group)], axis=1)

        def step(kb, dq):
            base = pl.multiple_of(kb * rows, rows)
            k = kv_scr[pl.ds(base, rows), k_lane : k_lane + HEAD_SIZE]
            v = kv_scr[pl.ds(base, rows), v_lane : v_lane + HEAD_SIZE]
            s = mm_nt(k, q)
            p = jnp.where(key_line + base <= bound, jnp.exp(s - shift), 0.0)
            ds = (p * (mm_nt(v, do) - slope)).astype(BF)
            dkv_scr[pl.ds(base, rows), v_lane : v_lane + HEAD_SIZE] = mm(p.astype(BF), do)
            dkv_scr[pl.ds(base, rows), k_lane : k_lane + HEAD_SIZE] = mm(ds, q)
            return dq + mm_tn(k, ds)

        dq = lax.fori_loop(0, count, step, jnp.zeros((HEAD_SIZE, group * rows), F32))
        for i in range(group):
            dq_scr[:, (lo + i) * HEAD_SIZE : (lo + i + 1) * HEAD_SIZE] = dq[
                :, i * rows : (i + 1) * rows
            ].T
    cosine = cos_ref[...]
    sine = -sin_ref[...]
    for j in range(0, q_width, LANES):
        dq_ref[:, j : j + LANES] = (
            spin(dq_scr[:, j : j + LANES], cosine, sine) * HEAD_SIZE ** (-0.5)
        ).astype(BF)
    for j in range(blocks):
        dkv_refs[j][...] = dkv_scr[
            pl.ds(pl.multiple_of(info[3 + j] * rows, rows), rows), :
        ].astype(BF)


def attend_back(info, q, kv_blocks, wo, o, lse, mine, other, cosine, sine):
    rows, q_width = q.shape
    width = wo.shape[1]
    blocks = len(kv_blocks)
    kv_width = kv_blocks[0].shape[1]
    half = rows // 2
    heads = q_width // HEAD_SIZE
    outs = pl.pallas_call(
        functools.partial(attend_back_kernel, blocks=blocks, tp_rows=half),
        out_shape=(jax.ShapeDtypeStruct((rows, q_width), BF),)
        + (jax.ShapeDtypeStruct((rows, kv_width), BF),) * blocks,
        in_specs=[smem()] + [vmem()] * (8 + blocks),
        out_specs=(vmem(),) * (1 + blocks),
        scratch_shapes=[
            pltpu.VMEM((blocks * rows, kv_width), BF),
            pltpu.VMEM((blocks * rows, kv_width), F32),
            pltpu.VMEM((rows, width), BF),
            pltpu.VMEM((rows, q_width), BF),
            pltpu.VMEM((rows, q_width), F32),
        ],
        cost_estimate=cost(10 * rows * rows * blocks * q_width * 4, 1.2e7, heads * rows * rows * blocks),
        name="attend_back",
    )(info, q, *kv_blocks, wo, o, lse, mine, other, cosine, sine)
    return outs[0], outs[1:]


def expert_kernel(
    info,
    table_ref,
    h_mine_ref,
    h_other_ref,
    d_mine_ref,
    d_other_ref,
    router_ref,
    wg_ref,
    wu_ref,
    wd_ref,
    moe_mine_ref,
    moe_other_ref,
    dh_mine_ref,
    dh_other_ref,
    xs_ref,
    dgu_ref,
    hid_ref,
    dy_ref,
    hd_scr,
    gate_scr,
    turn_scr,
    moe_scr,
    dh_scr,
):
    e = pl.program_id(0)
    last = pl.num_programs(0) - 1
    half, width = h_mine_ref.shape
    rows = 2 * half
    tp_index = info[0]
    own = pl.multiple_of(tp_index * half, half)
    far = pl.multiple_of((1 - tp_index) * half, half)
    index = info[1] + e

    @pl.when(e == 0)
    def _():
        hd_scr[pl.ds(own, half), :width] = h_mine_ref[...]
        hd_scr[pl.ds(far, half), :width] = h_other_ref[...]
        hd_scr[pl.ds(own, half), width:] = d_mine_ref[...]
        hd_scr[pl.ds(far, half), width:] = d_other_ref[...]
        table = table_ref[...]
        logits = mm_nt(router_ref[...], hd_scr[:, :width])
        logits = jnp.where(table > -1.5, logits, NEGATIVE)
        raised = jnp.exp(logits - jnp.max(logits, axis=0, keepdims=True))
        gate_scr[...] = raised / jnp.sum(raised, axis=0, keepdims=True)
        padded = jnp.concatenate([table, jnp.full((LANES - E, rows), -3.0, F32)], axis=0)
        turn_scr[...] = padded.T
        moe_scr[...] = jnp.zeros_like(moe_scr)
        dh_scr[...] = jnp.zeros_like(dh_scr)

    place_row = table_ref[pl.ds(index, 1), :]
    lane = lax.broadcasted_iota(jnp.int32, (rows, LANES), 1)
    place_col = jnp.sum(jnp.where(lane == index, turn_scr[...], 0.0), axis=1, keepdims=True)
    slot_col = lax.broadcasted_iota(jnp.int32, (CAP, rows), 0).astype(F32)
    slot_row = lax.broadcasted_iota(jnp.int32, (rows, CAP), 1).astype(F32)
    pick = jnp.where(slot_col == place_row, 1.0, 0.0)
    spread = jnp.where(slot_row == place_col, 1.0, 0.0).astype(BF)
    gate = jnp.sum(pick * gate_scr[pl.ds(index, 1), :], axis=1, keepdims=True)
    pick = pick.astype(BF)
    xs = mm(pick, hd_scr[:, :width]).astype(BF)
    xs_ref[0] = xs
    dsel = mm(pick, hd_scr[:, width:])
    wg = wg_ref[0]
    wu = wu_ref[0]
    wd = wd_ref[0]
    gpre = mm(xs, wg)
    upre = mm(xs, wu)
    sig = 1.0 / (1.0 + jnp.exp(-gpre))
    act = gpre * sig
    hid = (act * upre).astype(BF)
    hid_ref[0] = hid
    y = mm(hid, wd)
    dgate = jnp.sum(dsel * y, axis=1, keepdims=True)
    moe_scr[...] += mm(spread, (gate * y).astype(BF))
    dy = (gate * dsel).astype(BF)
    dy_ref[0] = dy
    dhid = mm_nt(dy, wd)
    dg = (dhid * upre * sig * (1.0 + gpre * (1.0 - sig))).astype(BF)
    du = (dhid * act).astype(BF)
    f = dg.shape[1]
    dgu_ref[0, :, :f] = dg
    dgu_ref[0, :, f:] = du
    dxs = (mm_nt(dg, wg) + mm_nt(du, wu)).astype(BF)
    tail = jnp.where(
        lax.broadcasted_iota(jnp.int32, (CAP, LANES), 1) == index, dgate, 0.0
    ).astype(BF)
    dh_scr[:, :width] += mm(spread, dxs)
    dh_scr[:, width:] += mm(spread, tail)

    @pl.when(e == last)
    def _():
        moe_mine_ref[...] = moe_scr[pl.ds(own, half), :].astype(BF)
        moe_other_ref[...] = moe_scr[pl.ds(far, half), :].astype(BF)
        dh_mine_ref[...] = dh_scr[pl.ds(own, half), :].astype(BF)
        dh_other_ref[...] = dh_scr[pl.ds(far, half), :].astype(BF)


def experts(info, table, h_mine, h_other, d_mine, d_other, router, wg, wu, wd):
    half, width = h_mine.shape
    count, _, f = wg.shape
    whole = lambda shape: pl.BlockSpec(shape, lambda e: (0,) * len(shape))
    per = lambda *shape: pl.BlockSpec((1,) + shape, lambda e: (e,) + (0,) * len(shape))
    tall = (half, width + LANES)
    return pl.pallas_call(
        expert_kernel,
        grid=(count,),
        out_shape=(
            jax.ShapeDtypeStruct((half, width), BF),
            jax.ShapeDtypeStruct((half, width), BF),
            jax.ShapeDtypeStruct(tall, BF),
            jax.ShapeDtypeStruct(tall, BF),
            jax.ShapeDtypeStruct((count, CAP, width), BF),
            jax.ShapeDtypeStruct((count, CAP, 2 * f), BF),
            jax.ShapeDtypeStruct((count, CAP, f), BF),
            jax.ShapeDtypeStruct((count, CAP, width), BF),
        ),
        in_specs=[
            smem(),
            whole(table.shape),
            whole((half, width)),
            whole((half, width)),
            whole((half, width)),
            whole((half, width)),
            whole(router.shape),
            per(width, f),
            per(width, f),
            per(f, width),
        ],
        out_specs=(
            whole((half, width)),
            whole((half, width)),
            whole(tall),
            whole(tall),
            per(CAP, width),
            per(CAP, 2 * f),
            per(CAP, f),
            per(CAP, width),
        ),
        scratch_shapes=[
            pltpu.VMEM((2 * half, 2 * width), BF),
            pltpu.VMEM((E, 2 * half), F32),
            pltpu.VMEM((2 * half, LANES), F32),
            pltpu.VMEM((2 * half, width), F32),
            pltpu.VMEM((2 * half, width + LANES), F32),
        ],
        compiler_params=pltpu.CompilerParams(dimension_semantics=("arbitrary",)),
        cost_estimate=cost(count * CAP * width * (2 * f * 6 + 4 * half * 2 * 2), 2.5e7),
        name="experts",
    )(info, table, h_mine, h_other, d_mine, d_other, router, wg, wu, wd)


def expert_grad_kernel(*refs, parts):
    xs_refs = refs[:parts]
    dgu_refs = refs[parts : 2 * parts]
    hid_refs = refs[2 * parts : 3 * parts]
    dy_refs = refs[3 * parts : 4 * parts]
    gate_ref, up_ref, down_ref = refs[4 * parts :]
    f = gate_ref.shape[2]
    total = mm_tn(xs_refs[0][0], dgu_refs[0][0])
    down = mm_tn(hid_refs[0][0], dy_refs[0][0])
    for i in range(1, parts):
        total = total + mm_tn(xs_refs[i][0], dgu_refs[i][0])
        down = down + mm_tn(hid_refs[i][0], dy_refs[i][0])
    gate_ref[0] = total[:, :f].astype(BF)
    up_ref[0] = total[:, f:].astype(BF)
    down_ref[0] = down.astype(BF)


def expert_grads(saved):
    parts = len(saved)
    count, _, width = saved[0][0].shape
    f = saved[0][2].shape[2]
    per = lambda *shape: pl.BlockSpec((1,) + shape, lambda e: (e,) + (0,) * len(shape))
    operands = [s[i] for i in range(4) for s in saved]
    return pl.pallas_call(
        functools.partial(expert_grad_kernel, parts=parts),
        grid=(count,),
        out_shape=(
            jax.ShapeDtypeStruct((count, width, f), BF),
            jax.ShapeDtypeStruct((count, width, f), BF),
            jax.ShapeDtypeStruct((count, f, width), BF),
        ),
        in_specs=[per(CAP, width)] * parts
        + [per(CAP, 2 * f)] * parts
        + [per(CAP, f)] * parts
        + [per(CAP, width)] * parts,
        out_specs=(per(width, f), per(width, f), per(f, width)),
        compiler_params=pltpu.CompilerParams(dimension_semantics=("arbitrary",)),
        cost_estimate=cost(parts * count * CAP * width * f * 6, 4e7),
        name="expert_grads",
    )(*operands)


def local(
    tokens,
    lengths,
    routes,
    visit_order,
    cotangent,
    first_gain,
    query_weight,
    key_matrix,
    value_matrix,
    output_weight,
    second_gain,
    router_weight,
    gate_weight,
    up_weight,
    down_weight,
    *,
    n_f,
    n_c,
):
    rows = tokens.shape[1]
    width = tokens.shape[2]
    half = rows // 2
    f_index = lax.axis_index("fsdp")
    c_index = lax.axis_index("ctx")
    t_index = lax.axis_index("tp")
    core = c_index % 2
    length = lengths[0]
    first_row = c_index * rows
    part = query_weight.shape[0]
    q_width = query_weight.shape[1]
    k_width = key_matrix.shape[1]
    kv_width = 2 * k_width

    ring_perm = [(i, (i + 1) % n_f) for i in range(n_f)]
    core_perm = [(i, i ^ 1) for i in range(n_c)]

    def z_next(v):
        return lax.ppermute(v, "fsdp", ring_perm)

    def z_home(v, k):
        return lax.ppermute(v, "fsdp", [(i, (i - k) % n_f) for i in range(n_f)])

    def core_swap(v):
        return lax.ppermute(v, "ctx", core_perm)

    def x_shift(v, j):
        return lax.ppermute(v, "ctx", [(i, (i + 2 * j) % n_c) for i in range(n_c)])

    def x_mix(v, bit):
        return lax.ppermute(v, "ctx", [(i, i ^ bit) for i in range(n_c)])

    def tp_swap(v):
        return lax.ppermute(v, "tp", [(0, 1), (1, 0)])

    def ring(v):
        pieces = [v]
        for _ in range(n_f - 1):
            pieces.append(z_next(pieces[-1]))
        return pieces

    def source(k):
        return (f_index - k) % n_f

    def join(mine, other):
        return jnp.where(
            t_index == 0,
            jnp.concatenate([mine, other], axis=0),
            jnp.concatenate([other, mine], axis=0),
        )

    def my_half(v):
        return lax.dynamic_slice_in_dim(v, t_index * half, half, 0)

    small = jnp.concatenate(
        [
            router_weight.T,
            first_gain[None],
            second_gain[None],
            jnp.zeros((14, part), BF),
        ],
        axis=0,
    )
    small_full = jnp.zeros((32, width), BF)
    for k, piece in enumerate(ring(small)):
        small_full = lax.dynamic_update_slice(small_full, piece, (0, source(k) * part))
    router_t = small_full[:E]
    gain_first = small_full[E : E + 1].astype(F32)
    gain_second = small_full[E + 1 : E + 2].astype(F32)

    q_half = q_width // 2
    k_half = k_width // 2
    qkv_part = jnp.concatenate(
        [
            lax.dynamic_slice_in_dim(query_weight, core * q_half, q_half, 1),
            lax.dynamic_slice_in_dim(key_matrix, core * k_half, k_half, 1),
            lax.dynamic_slice_in_dim(value_matrix, core * k_half, k_half, 1),
        ],
        axis=1,
    )
    qkv_full = jnp.zeros((2, width, q_half + 2 * k_half), BF)
    qkv_pieces = ring(qkv_part)
    for k, piece in enumerate(qkv_pieces):
        qkv_full = lax.dynamic_update_slice(qkv_full, piece[None], (core, source(k) * part, 0))
        qkv_full = lax.dynamic_update_slice(
            qkv_full, core_swap(piece)[None], (1 - core, source(k) * part, 0)
        )
    o_half = q_width // 2
    out_part = lax.dynamic_slice_in_dim(output_weight, core * o_half, o_half, 0)
    out_part, _ = lax.optimization_barrier((out_part, qkv_pieces[-1]))
    out_full = jnp.zeros((q_width, width), BF)
    out_pieces = ring(out_part)
    for k, piece in enumerate(out_pieces):
        out_full = lax.dynamic_update_slice(out_full, piece, (core * o_half, source(k) * part))
        out_full = lax.dynamic_update_slice(
            out_full, core_swap(piece), ((1 - core) * o_half, source(k) * part)
        )

    positions = first_row + jnp.arange(rows, dtype=jnp.int32)
    lane = jnp.arange(LANES, dtype=jnp.int32)
    frequency = jnp.exp((lane % HALF_HEAD).astype(F32) * (-2.0 * math.log(10000.0) / HEAD_SIZE))
    angles = positions.astype(F32)[:, None] * frequency[None, :]
    cosine = jnp.cos(angles)
    sine = jnp.sin(angles) * jnp.where(lane % HEAD_SIZE < HALF_HEAD, -1.0, 1.0)[None, :]

    plan_info = jnp.stack([first_row, length]).astype(jnp.int32)
    table = make_plan(plan_info, visit_order[0], routes[0].T)
    tables = ring(table)

    row_index = first_row + t_index * half + jnp.arange(half, dtype=jnp.int32)
    valid = (row_index < length).astype(F32)[:, None]
    d_low = (my_half(cotangent[0]).astype(F32) * valid).astype(BF)
    d_send, _ = lax.optimization_barrier((d_low, out_pieces[-1]))
    d_mine = ring(d_send)
    d_other = [tp_swap(v) for v in d_mine]

    hidden_one, q, kv = project(
        tokens[0], gain_first, qkv_full, cosine, sine, q_width, kv_width
    )
    kv_blocks = []
    kv_index = []
    moved = kv
    for j in range(n_c // 2):
        if j > 0:
            moved = x_shift(moved, 1)
        where = (c_index - 2 * j) % n_c
        kv_blocks += [moved, core_swap(moved)]
        kv_index += [where, where ^ 1]
    info = jnp.stack([c_index, length, t_index] + kv_index).astype(jnp.int32)
    o, lse, sum_mine, sum_other = attend(info, q, kv_blocks, out_full)
    inputs = my_half(tokens[0]).astype(F32)
    residual = inputs + sum_mine + tp_swap(sum_other).astype(F32)
    inverse_two = lax.rsqrt(jnp.mean(residual * residual, axis=-1, keepdims=True) + EPSILON)
    normed_two = residual * inverse_two
    hidden_two = (normed_two * gain_second).astype(BF)

    h_mine = ring(hidden_two)
    h_other = [tp_swap(v) for v in h_mine]
    count = gate_weight.shape[0]
    expert_info = jnp.stack([t_index, f_index * count]).astype(jnp.int32)
    saved = []
    moe_sum = None
    dh_sum = None
    for k in range(n_f):
        moe_a, moe_b, dh_a, dh_b, xs, dgu, hid, dy = experts(
            expert_info,
            tables[k],
            h_mine[k],
            h_other[k],
            d_mine[k],
            d_other[k],
            router_t,
            gate_weight,
            up_weight,
            down_weight,
        )
        saved.append((xs, dgu, hid, dy))
        dh = dh_a.astype(F32) + tp_swap(dh_b).astype(F32)
        moe = moe_a.astype(F32) + tp_swap(moe_b).astype(F32)
        if k > 0:
            dh = z_home(dh.astype(BF), k).astype(F32)
            moe = z_home(moe.astype(BF), k).astype(F32)
        dh_sum = dh if dh_sum is None else dh_sum + dh
        moe_sum = moe if moe_sum is None else moe_sum + moe

    out_mine = (valid * (residual + moe_sum)).astype(BF)
    layer_out = join(out_mine, tp_swap(out_mine))[None]

    grads = expert_grads(saved)

    def sum_ctx(grad, axis):
        size = grad.shape[axis] // 2
        keep = lax.dynamic_slice_in_dim(grad, core * size, size, axis)
        send = lax.dynamic_slice_in_dim(grad, (1 - core) * size, size, axis)
        total = keep.astype(F32) + core_swap(send).astype(F32)
        bit = 2
        while bit < n_c:
            low = total.astype(BF)
            total = low.astype(F32) + x_mix(low, bit).astype(F32)
            bit *= 2
        low = total.astype(BF)
        there = core_swap(low)
        return jnp.where(
            core == 0,
            jnp.concatenate([low, there], axis=axis),
            jnp.concatenate([there, low], axis=axis),
        ).astype(F32)

    grad_gate_w = sum_ctx(grads[0], 1)
    grad_up_w = sum_ctx(grads[1], 1)
    grad_down_w = sum_ctx(grads[2], 1)

    table_mine = lax.dynamic_slice_in_dim(table, t_index * half, half, 1)
    chosen = table_mine.T > -1.5
    logits = jnp.where(chosen, mm_nt(hidden_two, router_t), NEGATIVE)
    gates = jax.nn.softmax(logits, axis=-1)
    gate_grad = dh_sum[:, width : width + E]
    logit_grad = (
        gates * (gate_grad - jnp.sum(gates * gate_grad, axis=-1, keepdims=True))
    ).astype(BF)
    hidden_grad = dh_sum[:, :width] + mm(logit_grad, router_t)
    grad_router_t = mm_tn(logit_grad, hidden_two)
    grad_second = jnp.sum(hidden_grad * normed_two, axis=0, keepdims=True)
    scaled = hidden_grad * gain_second
    residual_grad = d_low.astype(F32) + inverse_two * (
        scaled - normed_two * jnp.mean(scaled * normed_two, axis=-1, keepdims=True)
    )
    branch_mine = residual_grad.astype(BF)
    branch_other = tp_swap(branch_mine)

    dq, dkv_blocks = attend_back(
        info, q, kv_blocks, out_full, o, lse, branch_mine, branch_other, cosine, sine
    )
    branch = join(branch_mine, branch_other)

    def scatter_f(grad, part_axis, core_axis):
        size = grad.shape[core_axis] // 2
        low = grad.astype(BF)
        keep = lax.dynamic_slice_in_dim(low, core * size, size, core_axis)
        send = lax.dynamic_slice_in_dim(low, (1 - core) * size, size, core_axis)
        total = (keep.astype(F32) + core_swap(send).astype(F32)).astype(BF)
        width_f = grad.shape[part_axis] // n_f
        mine = lax.dynamic_slice_in_dim(total, f_index * width_f, width_f, part_axis).astype(F32)
        for k in range(1, n_f):
            piece = lax.dynamic_slice_in_dim(total, source(k) * width_f, width_f, part_axis)
            mine = mine + z_home(piece, k).astype(F32)
        bit = 2
        while bit < n_c:
            near = mine.astype(BF)
            mine = near.astype(F32) + x_mix(near, bit).astype(F32)
            bit *= 2
        near = mine.astype(BF)
        there = core_swap(near)
        return jnp.where(
            core == 0,
            jnp.concatenate([near, there], axis=core_axis),
            jnp.concatenate([there, near], axis=core_axis),
        ).astype(F32)

    grad_output_w = scatter_f(mm_tn(o, branch), 1, 0)
    grad_query_w = scatter_f(mm_tn(hidden_one, dq), 0, 1)

    sent = core_swap(jnp.concatenate(dkv_blocks[1::2], axis=0)).astype(F32)
    dkv = None
    for j in range(n_c // 2):
        piece = dkv_blocks[2 * j].astype(F32) + sent[j * rows : (j + 1) * rows]
        if j > 0:
            piece = x_shift(piece.astype(BF), -j).astype(F32)
        dkv = piece if dkv is None else dkv + piece
    halves = dkv.reshape(rows, 2, 2, k_half)
    dk = halves[:, :, 0].reshape(rows, k_width // LANES, 2, 2, HALF_HEAD)
    dk_a, dk_b = dk[:, :, :, 0], dk[:, :, :, 1]
    cos_k = cosine[:, None, None, :HALF_HEAD]
    sin_k = sine[:, None, None, HALF_HEAD:HEAD_SIZE]
    dk = jnp.stack([dk_a * cos_k + dk_b * sin_k, dk_b * cos_k - dk_a * sin_k], axis=3)
    dk = dk.reshape(rows, k_width).astype(BF)
    dv = halves[:, :, 1].reshape(rows, k_width).astype(BF)
    grad_key_w = scatter_f(mm_tn(hidden_one, dk), 0, 1)
    grad_value_w = scatter_f(mm_tn(hidden_one, dv), 0, 1)

    dh1 = None
    for s in range(2):
        step = (
            mm_nt(dq[:, s * q_half : (s + 1) * q_half], qkv_full[s, :, :q_half])
            + mm_nt(dk[:, s * k_half : (s + 1) * k_half], qkv_full[s, :, q_half : q_half + k_half])
            + mm_nt(dv[:, s * k_half : (s + 1) * k_half], qkv_full[s, :, q_half + k_half :])
        )
        dh1 = step if dh1 is None else dh1 + step
    dh1_other = lax.dynamic_slice_in_dim(dh1, (1 - t_index) * half, half, 0).astype(BF)
    dh1 = my_half(dh1) + tp_swap(dh1_other).astype(F32)
    inverse_one = lax.rsqrt(jnp.mean(inputs * inputs, axis=-1, keepdims=True) + EPSILON)
    normed_one = inputs * inverse_one
    grad_first = jnp.sum(dh1 * normed_one, axis=0, keepdims=True)
    scaled_one = dh1 * gain_first
    grad_mine = residual_grad + inverse_one * (
        scaled_one - normed_one * jnp.mean(scaled_one * normed_one, axis=-1, keepdims=True)
    )
    grad_tokens = join(grad_mine, tp_swap(grad_mine.astype(BF)).astype(F32))[None]

    tiny = jnp.concatenate([grad_router_t, grad_first, grad_second, jnp.zeros((14, width), F32)])
    tiny = tiny + tp_swap(tiny)
    bit = 1
    while bit < n_c:
        tiny = tiny + x_mix(tiny, bit)
        bit *= 2
    bit = 1
    while bit < n_f:
        tiny = tiny + lax.ppermute(tiny, "fsdp", [(i, i ^ bit) for i in range(n_f)])
        bit *= 2
    tiny = lax.dynamic_slice_in_dim(tiny, f_index * part, part, 1)

    return (
        layer_out,
        grad_tokens,
        tiny[E],
        grad_query_w,
        grad_key_w,
        grad_value_w,
        grad_output_w,
        tiny[E + 1],
        tiny[:E].T,
        grad_gate_w,
        grad_up_w,
        grad_down_w,
    )


def solution(mesh):
    placed = (
        P("fsdp", "ctx", None),
        P("fsdp"),
        P("fsdp", "ctx", None),
        P("fsdp", "ctx", None),
        P("fsdp", "ctx", None),
        P("fsdp"),
        P("fsdp", "tp"),
        P("fsdp", "tp"),
        P("fsdp", "tp"),
        P("tp", "fsdp"),
        P("fsdp"),
        P("fsdp", None),
        P("fsdp", None, "tp"),
        P("fsdp", None, "tp"),
        P("fsdp", "tp", None),
    )
    body = functools.partial(local, n_f=mesh.shape["fsdp"], n_c=mesh.shape["ctx"])
    return jax.shard_map(
        body,
        mesh=mesh,
        in_specs=placed,
        out_specs=(
            P("fsdp", "ctx", None),
            P("fsdp", "ctx", None),
            P("fsdp"),
            P("fsdp", "tp"),
            P("fsdp", "tp"),
            P("fsdp", "tp"),
            P("tp", "fsdp"),
            P("fsdp"),
            P("fsdp", None),
            P("fsdp", None, "tp"),
            P("fsdp", None, "tp"),
            P("fsdp", "tp", None),
        ),
        check_vma=False,
    )
```
